32 devices in a mesh: old: 4 (over y, core), new: 8 (over z, x).
Axes of the slice: x: 2, y: 2, z: 4, core: 2. Of those that a mesh axis runs over, the one named last changes fastest.
Arguments:
- old_field: bfloat16 [3, 27, 98304], P(None, None, ('old', 'new')), may hold values from -6 to 6
- pair_dest: int32 [32768, 1], P(('old', 'new')), may hold values from 0 to 31; in each aligned block of 1024 rows (0 to 1023, 1024 to 2047, ...) at most 128 rows name the same one
- pair_new: int32 [32768], P(('old', 'new')), may hold values from 0 to 511
- pair_old: int32 [32768], P(('old', 'new')), may hold values from 0 to 3071
- pair_block: int32 [32768], P(('old', 'new')), may hold values from 0 to 3
- basis_old: bfloat16 [4, 27, 125], replicated, may hold values from -1.25 to 1.25
- basis_new: bfloat16 [4, 27, 125], replicated, may hold values from -0.5 to 0.5
- volume: float32 [2, 8, 1024], P(None, 'old', 'new'), may hold values from 0.25 to 36, as said below
Outputs:
- solution: float32 [3, 5, 16, 2048], P(None, None, 'old', 'new')
- residual: float32 [3, 5, 16, 2048], P(None, None, 'old', 'new')
The draws below stay inside these ranges and needn't reach their ends.
Inputs may be any that keep to these rules, and one draw needn't show every extreme that they name: `pair_dest`: a device's index is its position along old times the number of devices along new plus its position along new; in each device's block of 1024 pairs at most 128 name one destination. `pair_new`: local element number (x * 2 + y) * 128 + z within the destination's block. `pair_old`: old element within the block of the device that holds the pair. `volume`: positive element factors.
All inputs are finite; a program needn't handle non-finite values.
Results may differ from the reference program's by a relative error of at most 0.003.
Values may be sent and summed in bfloat16 or wider, within the bound.
A program may use at most 64 MiB of HBM per device.

```python
import math
import jax
import jax.numpy as jnp
import numpy as np
from jax import lax

EX = 2
CY = 2
CZ = 128
E_OLD_DEV = 3072
CAP = 128
QB = 4
NQ = 125
ITERS = 4
P_DEV = 1024
PAIRS = 32768
E_OLD = 98304
E_NEW_DEV = 512
NYE = 8
NZE = 1024
N_NEW = 8
DEVICES = 32


def draw_volume(key, part):
    key_rough = jax.random.fold_in(key, 7)
    y_position = jnp.arange(NYE, dtype=jnp.float32) / NYE
    z_position = jnp.arange(NZE, dtype=jnp.float32) / NZE
    growth = jnp.exp(math.log(3.0) * y_position)[None, :, None] * jnp.exp(math.log(3.0) * z_position)[None, None, :]
    spread = math.log(2.0)
    roughness = jnp.exp(jax.random.uniform(key_rough, (EX, NYE, NZE), jnp.float32, -spread, spread))
    return (roughness * growth).astype(jnp.float32)


def place_ends(drawn, own_key, smallest, high):
    extent = drawn.shape
    spot = [jax.random.randint(jax.random.fold_in(own_key, axis), (), 0, extent[axis]) for axis in range(len(extent))]
    drawn = drawn.at[tuple(spot)].set(smallest)
    longest = extent.index(max(extent))
    spot[longest] = (spot[longest] + 1) % extent[longest]
    return drawn.at[tuple(spot)].set(high)


def shard_levels(rng, dims, cuts, smallest, high):
    gain, own = 1.0, jax.random.fold_in(rng, 6)
    for dim, shards_of in cuts:
        draws = jnp.exp(jax.random.uniform(jax.random.fold_in(own, dim), (shards_of,), jnp.float32, smallest / len(cuts), high / len(cuts)))
        gain = gain * jnp.repeat(draws, dims[dim] // shards_of).reshape([-1 if axis == dim else 1 for axis in range(len(dims))])
    return gain


def shared_out(rng, own, number, rows, count, top, limit, skew):
    order = jax.random.permutation(rng, count)
    packed, usual = shares(count, rows * top, limit, skew, True), shares(count, rows * top, limit, skew, False)
    places = jnp.arange(count)

    def named(sizes, turn):
        used = int((sizes > 0).sum())
        fixed = max(1, used // 4)
        passed = fixed + (places - fixed + turn * (used - fixed)) % max(1, count - fixed)
        return jnp.zeros((count,), jnp.int32).at[order[jnp.where(places < fixed, places, passed)]].set(jnp.asarray(sizes, jnp.int32))

    sizes = jnp.where(number % 4 == 0, named(packed, number // 4), named(usual, number - number // 4 - 1))
    mixed = jax.random.permutation(jax.random.fold_in(own, 3), count)
    giver, taker = mixed[0:count // 2 * 2:2], mixed[1:count // 2 * 2:2]
    margin = jnp.minimum(sizes[giver] - 1, limit - sizes[taker]) // 2
    margin = jnp.where((giver == order[0]) | (taker == order[0]) | (sizes[taker] == 0), 0, jnp.maximum(margin, 0))
    passed = jax.random.randint(jax.random.fold_in(own, 4), (count // 2,), 0, 1 << 20) % (margin + 1)
    sizes = sizes.at[giver].add(-passed).at[taker].add(passed)
    members = jnp.searchsorted(jnp.cumsum(sizes), jnp.arange(rows * top), side="right").astype(jnp.int32)
    table = members.reshape(top, rows).T
    table = table[jax.random.permutation(jax.random.fold_in(own, 1), rows)]
    turn = jax.random.randint(jax.random.fold_in(own, 2), (rows, 1), 0, top)
    return jnp.take_along_axis(table, (jnp.arange(top)[None, :] + turn) % top, axis=1)


def shares(count, total, reach, lean, full):
    portions = [(1 << 20) // math.isqrt(standing ** lean) + 1 for standing in range(1, count + 1)]
    largest = reach if full else min(reach, max(-(-total // count), total * portions[0] // sum(portions)))
    least = 1 if total - largest >= count - 1 else 0
    given, spare = [largest] + [least] * (count - 1), total - largest - least * (count - 1)
    while spare > 0:
        movable = [i for i in range(1, count) if given[i] < largest] or [i for i in range(1, count) if given[i] < reach]
        whole, remaining = sum([portions[i] for i in movable]), spare
        for i in movable:
            addition = min(reach - given[i], max(1, remaining * portions[i] // whole), spare)
            given[i] = given[i] + addition
            spare = spare - addition
    return np.array(given)


def bell_draw(stream_key, shape, scale, limit, cuts=(), kind=jnp.bfloat16):
    result = jax.random.normal(stream_key, shape, jnp.float32) * scale
    if len(cuts) > 0:
        result = shard_levels(stream_key, shape, cuts, -0.22, 0.18) * result
    return jnp.clip(result, min=-limit, max=limit).astype(kind)


def setup_inputs(seed: int = 0) -> dict:
    key_of = jax.random.split(jax.random.key(seed), 9)
    old_field = bell_draw(key_of[0], (3, 27, E_OLD), 1.0, 6.0, ((2, 32),))
    pair_dest_keys = jax.random.split(jax.random.fold_in(key_of[1], 1), PAIRS // P_DEV)
    pair_dest_turns = jax.random.permutation(jax.random.fold_in(key_of[1], 3), PAIRS // P_DEV)
    pair_dest = jax.vmap(lambda own, number: shared_out(jax.random.fold_in(key_of[1], 2), own, number, P_DEV, DEVICES, 1, CAP, 2))(pair_dest_keys, pair_dest_turns).reshape((PAIRS, 1))
    pair_new = place_ends(jax.random.randint(key_of[2], (PAIRS,), 0, E_NEW_DEV), jax.random.fold_in(key_of[2], 1), 0, E_NEW_DEV - 1).astype(jnp.int32)
    pair_old = place_ends(jax.random.randint(key_of[3], (PAIRS,), 0, E_OLD_DEV), jax.random.fold_in(key_of[3], 1), 0, E_OLD_DEV - 1).astype(jnp.int32)
    pair_block = place_ends(jax.random.randint(key_of[4], (PAIRS,), 0, QB), jax.random.fold_in(key_of[4], 1), 0, QB - 1).astype(jnp.int32)
    basis_old = bell_draw(key_of[5], (QB, 27, NQ), 27 ** -0.5, 1.25)
    basis_new = bell_draw(key_of[6], (QB, 27, NQ), NQ ** -0.5, 0.5)
    volume = draw_volume(jax.random.fold_in(key_of[8], 71), 0)
    return dict(old_field=old_field, pair_dest=pair_dest, pair_new=pair_new, pair_old=pair_old, pair_block=pair_block, basis_old=basis_old, basis_new=basis_new, volume=volume)


LINE_MASS = np.array([[4.0, 2.0, -1.0], [2.0, 16.0, 2.0], [-1.0, 2.0, 4.0]]) / 15.0


def pick_nodes(extended, cell_counts):
    along_first, along_second, along_third = cell_counts
    pieces = []
    for a in range(3):
        for b in range(3):
            for c in range(3):
                pieces.append(extended[:, a:a + 2 * along_first:2, b:b + 2 * along_second:2, c:c + 2 * along_third:2])
    stacked = jnp.stack(pieces, axis=1)
    return stacked.reshape((3, 3, 3, 3) + tuple(cell_counts))


def element_mass(element_nodes, volume):
    line_mass = jnp.asarray(LINE_MASS, dtype=jnp.float32)
    high = lax.Precision.HIGHEST
    applied = jnp.einsum('ia,cabdxyz->cibdxyz', line_mass, element_nodes, precision=high)
    applied = jnp.einsum('jb,cibdxyz->cijdxyz', line_mass, applied, precision=high)
    applied = jnp.einsum('kd,cijdxyz->cijkxyz', line_mass, applied, precision=high)
    return applied * volume


def spread_nodes(element_nodes):
    summed = None
    zero_value = jnp.zeros((), element_nodes.dtype)
    for a in range(3):
        for b in range(3):
            for c in range(3):
                padded = lax.pad(element_nodes[:, a, b, c], zero_value, ((0, 0, 0), (a, 2 - a, 1), (b, 2 - b, 1), (c, 2 - c, 1)))
                summed = padded if summed is None else summed + padded
    return summed


def fold_rims(assembled):
    inner_part = assembled[..., :-1]
    inner_part = jnp.concatenate([inner_part[..., :1] + assembled[..., -1:], inner_part[..., 1:]], axis=3)
    folded = inner_part[:, :, :-1]
    folded = jnp.concatenate([folded[:, :, :1] + inner_part[:, :, -1:], folded[:, :, 1:]], axis=2)
    return folded


def operate(vector, volume):
    extended = jnp.concatenate([vector, vector[:, :, :1]], axis=2)
    extended = jnp.concatenate([extended, extended[..., :1]], axis=3)
    element_nodes = pick_nodes(extended, volume.shape)
    return fold_rims(spread_nodes(element_mass(element_nodes, volume)))


def reference(old_field, pair_dest, pair_new, pair_old, pair_block, basis_old, basis_new, volume):
    destination = pair_dest[:, 0].reshape(DEVICES, P_DEV)
    new_local = pair_new.reshape(DEVICES, P_DEV)
    old_local = pair_old.reshape(DEVICES, P_DEV)
    block_kind = pair_block.reshape(DEVICES, P_DEV)

    def add_block(accumulated, inputs):
        block_index, dest_row, new_row, old_row, kind_row = inputs
        gathered = jnp.take(old_field, block_index * E_OLD_DEV + old_row, axis=2)
        chosen_old = jnp.take(basis_old, kind_row, axis=0).astype(jnp.float32)
        chosen_new = jnp.take(basis_new, kind_row, axis=0).astype(jnp.float32)
        values = jnp.einsum('cap,pak->ckp', gathered.astype(jnp.float32), chosen_old).astype(jnp.bfloat16)
        contribution = jnp.einsum('ckp,pak->cap', values.astype(jnp.float32), chosen_new)
        old_position = dest_row // N_NEW
        new_position = dest_row % N_NEW
        first_cell = new_row // (CY * CZ)
        second_cell = old_position * CY + (new_row // CZ) % CY
        third_cell = new_position * CZ + new_row % CZ
        flat_index = ((first_cell * NYE + second_cell) * NZE + third_cell).astype(jnp.int32)
        return accumulated.at[:, flat_index].add(contribution.reshape(81, -1)), None

    starting = jnp.zeros((81, EX * NYE * NZE), jnp.float32)
    sequence = (jnp.arange(DEVICES, dtype=jnp.int32), destination, new_local, old_local, block_kind)
    element_load, _ = lax.scan(add_block, starting, sequence)
    load_vector = fold_rims(spread_nodes(element_load.reshape(3, 3, 3, 3, EX, NYE, NZE)))

    solution = jnp.zeros_like(load_vector)
    residual = load_vector
    direction = load_vector
    norm_now = jnp.sum(residual * residual, axis=(1, 2, 3))
    for iteration in range(ITERS):
        applied = operate(direction, volume)
        step_size = norm_now / jnp.sum(direction * applied, axis=(1, 2, 3))
        solution = solution + step_size[:, None, None, None] * direction
        residual = residual - step_size[:, None, None, None] * applied
        norm_next = jnp.sum(residual * residual, axis=(1, 2, 3))
        direction = residual + (norm_next / norm_now)[:, None, None, None] * direction
        norm_now = norm_next
    return solution, residual
```

```python
import functools
import math

import jax
import jax.numpy as jnp
from jax import lax
from jax.experimental import pallas as pl
from jax.experimental.pallas import tpu as pltpu
from jax.sharding import PartitionSpec as P

ITERS = 4
MESH = pl.DeviceIdType.MESH
VMEM = pltpu.VMEM
STRIDE = 32
ROWS = 3 * STRIDE
KINDS_AT = 27
F32 = jnp.float32
BF16 = jnp.bfloat16


def pack_kernel(devices, cap, dest_ref, new_ref, old_idx_ref, block_ref, field_ref, out_ref, square, rows, slots, count):
    lanes = rows.shape[1]
    old_elements = field_ref.shape[2]
    square[...] = jnp.zeros_like(square)

    def turn(j, carry):
        at = pl.ds(pl.multiple_of(j * lanes, lanes), lanes)
        for c in range(3):
            square[c * STRIDE : c * STRIDE + 27, :] = field_ref[c, :, at].astype(F32)
        rows[at, :] = square[...].T
        return carry

    lax.fori_loop(0, old_elements // lanes, turn, 0)
    slots[...] = jnp.zeros_like(slots)

    def clear(d, carry):
        count[d] = 0
        return carry

    lax.fori_loop(0, devices, clear, 0)
    lane = lax.broadcasted_iota(jnp.int32, (1, lanes), 1)

    def place(p, carry):
        d = dest_ref[p]
        rank = count[d]
        count[d] = rank + 1
        code = (new_ref[p] * 4 + block_ref[p]).astype(F32)
        row = rows[pl.ds(old_idx_ref[p], 1), :]
        slots[pl.ds(d * cap + rank, 1), :] = jnp.where(lane == KINDS_AT, code, row)
        return carry

    lax.fori_loop(0, dest_ref.shape[0], place, 0, unroll=8)

    row_at = lax.broadcasted_iota(jnp.int32, (ROWS, cap), 0)

    def send_form(d, carry):
        block = slots[pl.ds(pl.multiple_of(d * cap, cap), cap), :].T[:ROWS]
        code = block[KINDS_AT : KINDS_AT + 1].astype(jnp.int32)
        high = (code // 512).astype(F32)
        low = ((code // 4) % 128).astype(F32)
        kind = (code % 4).astype(F32)
        block = jnp.where(row_at == KINDS_AT, high, block)
        block = jnp.where(row_at == KINDS_AT + 1, low, block)
        block = jnp.where(row_at == KINDS_AT + 2, kind, block)
        out_ref[d] = block.astype(BF16)
        return carry

    lax.fori_loop(0, devices, send_form, 0)


def exchange_kernel(olds, news, cap, out_ref, in_ref, send_sem, recv_sem, own_sem):
    i, j = lax.axis_index("old"), lax.axis_index("new")
    me = i * news + j
    peers = [(a, b) for a in range(olds) for b in range(news) if a or b]
    barrier = pltpu.get_barrier_semaphore()
    for a, b in peers:
        pl.semaphore_signal(barrier, inc=1, device_id=((i + a) % olds, (j + b) % news), device_id_type=MESH)
    own_at = pl.ds(pl.multiple_of(me * cap, cap), cap)
    own = pltpu.make_async_copy(out_ref.at[me], in_ref.at[:, own_at], own_sem)
    own.start()
    pl.semaphore_wait(barrier, len(peers))
    copies = []
    for n, (a, b) in enumerate(peers):
        target = ((i + a) % olds, (j + b) % news)
        copy = pltpu.make_async_remote_copy(
            src_ref=out_ref.at[target[0] * news + target[1]],
            dst_ref=in_ref.at[:, own_at],
            send_sem=send_sem.at[n],
            recv_sem=recv_sem.at[n],
            device_id=target,
            device_id_type=MESH,
        )
        copy.start()
        copies.append(copy)
    own.wait()
    for copy in copies:
        copy.wait()


def row_of(big_x, a2, a3, c):
    return ((big_x * 3 + a2) * 3 + a3) * 3 + c


def load_kernel(cells, chunk, in_ref, old_ref, new_ref, volume_ref, pay_ref, square, first, second, total, load):
    kinds, _, points = old_ref.shape
    wide = square.shape[1] // 3
    elements = cells[0] * cells[1] * cells[2]
    for source in (old_ref, new_ref):
        square[...] = jnp.zeros_like(square)
        for q in range(kinds):
            for c in range(3):
                at = q * ROWS + c * STRIDE
                square[at : at + 27, c * wide : c * wide + points] = source[q].astype(F32)
        if source is old_ref:
            first[...] = square[...].T.astype(BF16)
        else:
            second[...] = square[...].astype(BF16)
    total[...] = jnp.zeros_like(total)

    def step(s, carry):
        at = pl.ds(pl.multiple_of(s * chunk, chunk), chunk)
        block = in_ref[:, at].astype(F32)
        kind = block[KINDS_AT + 2 : KINDS_AT + 3]
        element = (block[KINDS_AT : KINDS_AT + 1] * 128.0 + block[KINDS_AT + 1 : KINDS_AT + 2]).astype(jnp.int32)
        chosen = jnp.concatenate([jnp.where(kind == q, block, 0.0) for q in range(kinds)], axis=0).astype(BF16)
        values = jnp.dot(first[...], chosen, preferred_element_type=F32).astype(BF16)
        every = jnp.dot(second[...], values, preferred_element_type=F32)
        part = jnp.zeros((ROWS, chunk), F32)
        for q in range(kinds):
            part = part + jnp.where(kind == q, every[q * ROWS : (q + 1) * ROWS], 0.0)
        high = part.astype(BF16)
        low = (part - high.astype(F32)).astype(BF16)
        onehot = jnp.where(
            lax.broadcasted_iota(jnp.int32, (elements, chunk), 0) == element, 1.0, 0.0
        ).astype(BF16)
        total[...] += lax.dot_general(
            jnp.concatenate([high, low], axis=0), onehot, (((1,), (1,)), ((), ())), preferred_element_type=F32
        )
        return carry

    lax.fori_loop(0, in_ref.shape[1] // chunk, step, 0)
    load[...] = total[:ROWS] + total[ROWS:]
    for big_x in range(2 * cells[0] + 1):
        for a2 in range(3):
            for a3 in range(3):
                for c in range(3):
                    for y in range(cells[1]):
                        value = None
                        for x in range(cells[0]):
                            a1 = big_x - 2 * x
                            if 0 <= a1 <= 2:
                                r = c * STRIDE + a1 * 9 + a2 * 3 + a3
                                z = (x * cells[1] + y) * cells[2]
                                term = load[r : r + 1, z : z + cells[2]]
                                value = term if value is None else value + term
                        pay_ref[row_of(big_x, a2, a3, c), y : y + 1, :] = value
    for x in range(cells[0]):
        pay_ref[row_of(2 * cells[0] + 1, 0, 0, 0) + x] = volume_ref[x]


def line(a, b, c):
    ends = 2.0 * b
    return 4.0 * a + ends - c, 2.0 * (a + c) + 16.0 * b, 4.0 * c + ends - a


def solve_kernel(olds, news, cells, pay_ref, sol_ref, res_ref, around, volume, vec, prod, way, way_m, ans, parts, sums,
                 send_sem, recv_sem, sum_send, sum_recv):
    i, j = lax.axis_index("old"), lax.axis_index("new")
    cx, cy, cz = cells
    nodes_x = 2 * cx + 1
    ny = olds * cy
    volume_at = row_of(nodes_x, 0, 0, 0)
    near = [(a, b) for a in range(olds) for b in (0, 1, news - 1) if a or b]
    ring = [(0, b) for b in range(1, news)]
    barrier = pltpu.get_barrier_semaphore()
    greeted = near + [peer for peer in ring if peer not in near]
    for a, b in greeted:
        pl.semaphore_signal(barrier, inc=1, device_id=((i + a) % olds, (j + b) % news), device_id_type=MESH)
    around[i, 0] = pay_ref[...]
    pl.semaphore_wait(barrier, len(greeted))
    copies = []
    for n, (a, b) in enumerate(near):
        place = {0: 0, 1: 2, news - 1: 1}[b]
        copy = pltpu.make_async_remote_copy(
            src_ref=pay_ref,
            dst_ref=around.at[i, place],
            send_sem=send_sem.at[n],
            recv_sem=recv_sem.at[n],
            device_id=((i + a) % olds, (j + b) % news),
            device_id_type=MESH,
        )
        copy.start()
        copies.append(copy)
    for copy in copies:
        copy.wait()

    ghost_next = lax.broadcasted_iota(jnp.int32, (1, 1, cz), 2) < cz // 2

    def joined(first, count):
        pieces = []
        for a in range(olds):
            rows = pl.ds(first, count)
            ghost = jnp.where(ghost_next, around[a, 1, rows], around[a, 2, rows])
            pieces.append(jnp.concatenate([around[a, 0, rows], ghost], axis=2))
        return jnp.concatenate(pieces, axis=1)

    def up_y(v):
        return pltpu.roll(v, 1, v.ndim - 2)

    def up_z(v):
        return pltpu.roll(v, 1, v.ndim - 1)

    def down_y(v):
        return pltpu.roll(v, v.shape[-2] - 1, v.ndim - 2)

    def down_z(v):
        return pltpu.roll(v, v.shape[-1] - 1, v.ndim - 1)

    volume[...] = joined(volume_at, cx) * (1.0 / 3375.0)

    def assemble(big_x, carry):
        part = [[joined(row_of(big_x, a2, a3, 0), 3) for a3 in range(3)] for a2 in range(3)]
        flat = [[part[a2][0] + up_z(part[a2][2]), part[a2][1]] for a2 in range(3)]
        for q in range(2):
            vec[q, big_x] = flat[0][q] + up_y(flat[2][q])
            vec[2 + q, big_x] = flat[1][q]
        return carry

    lax.fori_loop(0, nodes_x, assemble, 0)

    def mass(c):
        gathered = {}

        def node(big_x, a2, a3):
            v = vec[(a2 % 2) * 2 + a3 % 2, big_x, c]
            if a2 == 2:
                v = down_y(v)
            if a3 == 2:
                v = down_z(v)
            return v

        for big_x in range(nodes_x):
            grid = [[node(big_x, a2, a3) for a3 in range(3)] for a2 in range(3)]
            grid = [line(*grid[a2]) for a2 in range(3)]
            grid = list(zip(*[line(grid[0][a3], grid[1][a3], grid[2][a3]) for a3 in range(3)]))
            gathered[big_x] = grid
        out = {}
        for a2 in range(3):
            for a3 in range(3):
                for x in range(cx):
                    ends = line(*[gathered[2 * x + a1][a2][a3] for a1 in range(3)])
                    for a1 in range(3):
                        term = ends[a1] * volume[x]
                        key = (2 * x + a1, a2, a3)
                        out[key] = out[key] + term if key in out else term
        for big_x in range(nodes_x):
            flat = [[out[big_x, a2, 0] + up_z(out[big_x, a2, 2]), out[big_x, a2, 1]] for a2 in range(3)]
            for q in range(2):
                prod[q, big_x, c] = flat[0][q] + up_y(flat[2][q])
                prod[2 + q, big_x, c] = flat[1][q]

    parts[...] = jnp.zeros_like(parts)
    norm_before, step_before = None, None
    for turn in range(ITERS):

        def apply(c, carry):
            mass(c)
            return carry

        lax.fori_loop(0, 3, apply, 0)
        for c in range(3):
            square = jnp.zeros((ny, cz), F32)
            cross = jnp.zeros((ny, cz), F32)
            for q in range(4):
                for big_x in range(nodes_x):
                    r = vec[q, big_x, c, :, :cz]
                    square = square + r * r
                    cross = cross + r * prod[q, big_x, c, :, :cz]
            parts[turn, c : c + 1, :] = jnp.sum(square, axis=0, keepdims=True)
            parts[turn, 3 + c : 4 + c, :] = jnp.sum(cross, axis=0, keepdims=True)
        copies = []
        for n, (a, b) in enumerate(ring):
            copy = pltpu.make_async_remote_copy(
                src_ref=parts.at[turn],
                dst_ref=sums.at[turn, j],
                send_sem=sum_send.at[turn, n],
                recv_sem=sum_recv.at[turn, n],
                device_id=(i, (j + b) % news),
                device_id_type=MESH,
            )
            copy.start()
            copies.append(copy)
        sums[turn, j] = parts[turn]
        for copy in copies:
            copy.wait()
        whole = sums[turn, 0]
        for b in range(1, news):
            whole = whole + sums[turn, b]
        whole = jnp.sum(whole, axis=1, keepdims=True)
        norm_now, cross_now = whole[0:3], whole[3:6]
        if turn == 0:
            step_size = norm_now / cross_now
            share = None
        else:
            share = norm_now / norm_before
            step_size = norm_now / (cross_now - share * norm_now / step_before)
        for c in range(3):
            alpha = step_size[c : c + 1]
            for q in range(4):
                for big_x in range(nodes_x):
                    at = (q, big_x, c)
                    r, w = vec[at], prod[at]
                    if turn > 0:
                        r_way = r + share[c : c + 1] * way[at]
                        w_way = w + share[c : c + 1] * way_m[at]
                        moved = ans[at] + alpha * r_way[:, :cz]
                    else:
                        r_way, w_way = r, w
                        moved = alpha * r[:, :cz]
                    way[at] = r_way
                    way_m[at] = w_way
                    ans[at] = moved
                    vec[at] = r - alpha * w_way
        norm_before, step_before = norm_now, step_size
    for source, target in ((ans, sol_ref), (vec, res_ref)):
        for a in range(olds):
            @pl.when(i == a)
            def _():
                target[...] = source[:, :, :, a * cy : (a + 1) * cy, :cz]


def on_device(olds, news, old_field, pair_dest, pair_new, pair_old, pair_block, basis_old, basis_new, volume):
    devices = olds * news
    pairs = pair_dest.shape[0]
    cap = 4 * pairs // devices
    cells = volume.shape
    elements = math.prod(cells)
    smem = pl.BlockSpec(memory_space=pltpu.SMEM)
    vmem = pl.BlockSpec(memory_space=VMEM)
    outgoing = pl.pallas_call(
        functools.partial(pack_kernel, devices, cap),
        out_shape=jax.ShapeDtypeStruct((devices, ROWS, cap), BF16),
        in_specs=[smem] * 4 + [vmem],
        out_specs=vmem,
        scratch_shapes=[
            VMEM((128, 128), F32),
            VMEM((old_field.shape[2], 128), F32),
            VMEM((devices * cap, 128), F32),
            pltpu.SMEM((devices,), jnp.int32),
        ],
        name="pack",
    )(pair_dest.reshape(-1), pair_new, pair_old, pair_block, old_field)
    arrived = pl.pallas_call(
        functools.partial(exchange_kernel, olds, news, cap),
        out_shape=jax.ShapeDtypeStruct((ROWS, devices * cap), BF16),
        in_specs=[vmem],
        out_specs=vmem,
        scratch_shapes=[
            pltpu.SemaphoreType.DMA((devices,)),
            pltpu.SemaphoreType.DMA((devices,)),
            pltpu.SemaphoreType.DMA,
        ],
        compiler_params=pltpu.CompilerParams(collective_id=0, has_side_effects=True),
        name="exchange",
    )(outgoing)
    kinds = basis_old.shape[0]
    wide = 128 * pl.cdiv(basis_old.shape[2], 128)
    chunk = 4 * 128
    pay_rows = row_of(2 * cells[0] + 1, 0, 0, 0) + cells[0]
    payload = pl.pallas_call(
        functools.partial(load_kernel, cells, chunk),
        out_shape=jax.ShapeDtypeStruct((pay_rows,) + cells[1:], F32),
        in_specs=[vmem] * 4,
        out_specs=vmem,
        scratch_shapes=[
            VMEM((kinds * ROWS, 3 * wide), F32),
            VMEM((3 * wide, kinds * ROWS), BF16),
            VMEM((kinds * ROWS, 3 * wide), BF16),
            VMEM((2 * ROWS, elements), F32),
            VMEM((ROWS, elements), F32),
        ],
        name="load",
    )(arrived, basis_old, basis_new, volume)
    nodes_x = 2 * cells[0] + 1
    ny, cz = olds * cells[1], cells[2]
    grid = (4, nodes_x, 3)
    own = jax.ShapeDtypeStruct(grid + cells[1:], F32)
    near = 3 * olds
    solved = pl.pallas_call(
        functools.partial(solve_kernel, olds, news, cells),
        out_shape=(own, own),
        in_specs=[vmem],
        out_specs=(vmem, vmem),
        scratch_shapes=[
            VMEM((olds, 3, pay_rows) + cells[1:], F32),
            VMEM((cells[0], ny, 2 * cz), F32),
            VMEM(grid + (ny, 2 * cz), F32),
            VMEM(grid + (ny, 2 * cz), F32),
            VMEM(grid + (ny, 2 * cz), F32),
            VMEM(grid + (ny, 2 * cz), F32),
            VMEM(grid + (ny, cz), F32),
            VMEM((ITERS, 8, cz), F32),
            VMEM((ITERS, news, 8, cz), F32),
            pltpu.SemaphoreType.DMA((near,)),
            pltpu.SemaphoreType.DMA((near,)),
            pltpu.SemaphoreType.DMA((ITERS, news)),
            pltpu.SemaphoreType.DMA((ITERS, news)),
        ],
        compiler_params=pltpu.CompilerParams(collective_id=1, has_side_effects=True),
        name="solve",
    )(payload)

    def woven(v):
        v = v.reshape((2, 2) + v.shape[1:])
        v = jnp.transpose(v, (3, 2, 4, 0, 5, 1))
        return v.reshape(3, nodes_x, 2 * cells[1], 2 * cz)

    return woven(solved[0]), woven(solved[1])


def solution(mesh):
    in_specs = (
        P(None, None, ("old", "new")),
        P(("old", "new"), None),
        P(("old", "new")),
        P(("old", "new")),
        P(("old", "new")),
        P(),
        P(),
        P(None, "old", "new"),
    )
    out_specs = (P(None, None, "old", "new"), P(None, None, "old", "new"))
    return jax.shard_map(
        functools.partial(on_device, mesh.shape["old"], mesh.shape["new"]),
        mesh=mesh,
        in_specs=in_specs,
        out_specs=out_specs,
        check_vma=False,
    )
```

```python
import functools
import math

import jax
import jax.numpy as jnp
from jax import lax
from jax.experimental import pallas as pl
from jax.experimental.pallas import tpu as pltpu
from jax.sharding import PartitionSpec as P

MESH = pl.DeviceIdType.MESH
VMEM = pltpu.VMEM
STRIDE = 32
ROWS = 3 * STRIDE
EDGE = 8
KINDS_AT = 27
F32 = jnp.float32
BF16 = jnp.bfloat16


def pack_kernel(devices, cap, dest_ref, new_ref, old_idx_ref, block_ref, field_ref, out_ref, square, rows, slots, count):
    lanes = rows.shape[1]
    old_elements = field_ref.shape[2]
    square[...] = jnp.zeros_like(square)

    def turn(j, carry):
        at = pl.ds(pl.multiple_of(j * lanes, lanes), lanes)
        for c in range(3):
            square[c * STRIDE : c * STRIDE + 27, :] = field_ref[c, :, at].astype(F32)
        rows[at, :] = square[...].T
        return carry

    lax.fori_loop(0, old_elements // lanes, turn, 0)
    slots[...] = jnp.zeros_like(slots)

    def clear(d, carry):
        count[d] = 0
        return carry

    lax.fori_loop(0, devices, clear, 0)
    lane = lax.broadcasted_iota(jnp.int32, (1, lanes), 1)

    def place(p, carry):
        d = dest_ref[p]
        rank = count[d]
        count[d] = rank + 1
        code = (new_ref[p] * 4 + block_ref[p]).astype(F32)
        row = rows[pl.ds(old_idx_ref[p], 1), :]
        slots[pl.ds(d * cap + rank, 1), :] = jnp.where(lane == KINDS_AT, code, row)
        return carry

    lax.fori_loop(0, dest_ref.shape[0], place, 0, unroll=8)

    row_at = lax.broadcasted_iota(jnp.int32, (ROWS, cap), 0)

    def send_form(d, carry):
        block = slots[pl.ds(pl.multiple_of(d * cap, cap), cap), :].T[:ROWS]
        code = block[KINDS_AT : KINDS_AT + 1].astype(jnp.int32)
        high = (code // 512).astype(F32)
        low = ((code // 4) % 128).astype(F32)
        kind = (code % 4).astype(F32)
        block = jnp.where(row_at == KINDS_AT, high, block)
        block = jnp.where(row_at == KINDS_AT + 1, low, block)
        block = jnp.where(row_at == KINDS_AT + 2, kind, block)
        out_ref[d] = block.astype(BF16)
        return carry

    lax.fori_loop(0, devices, send_form, 0)


def exchange_kernel(olds, news, cap, out_ref, in_ref, send_sem, recv_sem, own_sem):
    i, j = lax.axis_index("old"), lax.axis_index("new")
    me = i * news + j
    peers = [(a, b) for a in range(olds) for b in range(news) if a or b]
    barrier = pltpu.get_barrier_semaphore()
    for a, b in peers:
        pl.semaphore_signal(barrier, inc=1, device_id=((i + a) % olds, (j + b) % news), device_id_type=MESH)
    own_at = pl.ds(pl.multiple_of(me * cap, cap), cap)
    own = pltpu.make_async_copy(out_ref.at[me], in_ref.at[:, own_at], own_sem)
    own.start()
    pl.semaphore_wait(barrier, len(peers))
    copies = []
    for n, (a, b) in enumerate(peers):
        target = ((i + a) % olds, (j + b) % news)
        copy = pltpu.make_async_remote_copy(
            src_ref=out_ref.at[target[0] * news + target[1]],
            dst_ref=in_ref.at[:, own_at],
            send_sem=send_sem.at[n],
            recv_sem=recv_sem.at[n],
            device_id=target,
            device_id_type=MESH,
        )
        copy.start()
        copies.append(copy)
    own.wait()
    for copy in copies:
        copy.wait()


def row_of(big_x, a2, a3, c):
    return ((big_x * 3 + a2) * 3 + a3) * 3 + c


def load_kernel(cells, chunk, in_ref, old_ref, new_ref, volume_ref, pay_ref, edge_ref, square, first, second, total, load):
    _, kinds, points = old_ref.shape
    wide = square.shape[1] // 3
    elements = cells[0] * cells[1] * cells[2]
    for source in (old_ref, new_ref):
        square[...] = jnp.zeros_like(square)
        for q in range(kinds):
            for c in range(3):
                at = q * ROWS + c * STRIDE
                square[at : at + 27, c * wide : c * wide + points] = source[:, q].astype(F32)
        if source is old_ref:
            first[...] = square[...].T.astype(BF16)
        else:
            second[...] = square[...].astype(BF16)
    total[...] = jnp.zeros_like(total)

    def step(s, carry):
        at = pl.ds(pl.multiple_of(s * chunk, chunk), chunk)
        block = in_ref[:, at].astype(F32)
        kind = block[KINDS_AT + 2 : KINDS_AT + 3]
        element = (block[KINDS_AT : KINDS_AT + 1] * 128.0 + block[KINDS_AT + 1 : KINDS_AT + 2]).astype(jnp.int32)
        chosen = jnp.concatenate([jnp.where(kind == q, block, 0.0) for q in range(kinds)], axis=0).astype(BF16)
        values = jnp.dot(first[...], chosen, preferred_element_type=F32).astype(BF16)
        every = jnp.dot(second[...], values, preferred_element_type=F32)
        part = jnp.zeros((ROWS, chunk), F32)
        for q in range(kinds):
            part = part + jnp.where(kind == q, every[q * ROWS : (q + 1) * ROWS], 0.0)
        high = part.astype(BF16)
        low = (part - high.astype(F32)).astype(BF16)
        onehot = jnp.where(
            lax.broadcasted_iota(jnp.int32, (elements, chunk), 0) == element, 1.0, 0.0
        ).astype(BF16)
        total[...] += lax.dot_general(
            jnp.concatenate([high, low], axis=0), onehot, (((1,), (1,)), ((), ())), preferred_element_type=F32
        )
        return carry

    lax.fori_loop(0, in_ref.shape[1] // chunk, step, 0)
    load[...] = total[:ROWS] + total[ROWS:]
    for big_x in range(2 * cells[0] + 1):
        for a2 in range(3):
            for a3 in range(3):
                for c in range(3):
                    for y in range(cells[1]):
                        value = None
                        for x in range(cells[0]):
                            a1 = big_x - 2 * x
                            if 0 <= a1 <= 2:
                                r = c * STRIDE + a1 * 9 + a2 * 3 + a3
                                z = (x * cells[1] + y) * cells[2]
                                term = load[r : r + 1, z : z + cells[2]]
                                value = term if value is None else value + term
                        pay_ref[row_of(big_x, a2, a3, c), y : y + 1, :] = value
    for x in range(cells[0]):
        pay_ref[row_of(2 * cells[0] + 1, 0, 0, 0) + x] = volume_ref[x]
    group, cz = edge_ref.shape[1], cells[2]
    for r in range(row_of(2 * cells[0] + 1, 0, 0, 0) + cells[0], pay_ref.shape[0]):
        pay_ref[r] = jnp.zeros(cells[1:], F32)
    lane = lax.broadcasted_iota(jnp.int32, (1, 1, cz), 2)
    first_cells = jnp.zeros(edge_ref.shape[1:], F32)
    last_cells = jnp.zeros(edge_ref.shape[1:], F32)
    for t in range(cz // EDGE):
        rows = pay_ref[t * group : (t + 1) * group]
        here = lane // EDGE == t
        first_cells = jnp.where(here, pltpu.roll(rows, EDGE * t, 2), first_cells)
        last_cells = jnp.where(here, pltpu.roll(rows, (EDGE * t + EDGE) % cz, 2), last_cells)
    edge_ref[0] = first_cells
    edge_ref[1] = last_cells


def line(a, b, c):
    ends = 2.0 * b
    return 4.0 * a + ends - c, 2.0 * (a + c) + 16.0 * b, 4.0 * c + ends - a


def solve_kernel(olds, news, cells, pay_ref, edge_ref, sol_ref, res_ref, around, edges, ghost, volume, b0, b1, b2, b3, b4,
                 ans, parts, sums, woven, send_sem, recv_sem, edge_send, edge_recv, sum_send, sum_recv):
    i, j = lax.axis_index("old"), lax.axis_index("new")
    cx, cy, cz = cells
    nodes_x = 2 * cx + 1
    ny = olds * cy
    volume_at = row_of(nodes_x, 0, 0, 0)
    column = [(a, 0) for a in range(1, olds)]
    sides = [(a, b) for b in (1, news - 1) for a in range(olds)]
    ring = [(0, b) for b in range(1, news)]
    barrier = pltpu.get_barrier_semaphore()
    greeted = column + sides + [peer for peer in ring if peer not in sides]
    for a, b in greeted:
        pl.semaphore_signal(barrier, inc=1, device_id=((i + a) % olds, (j + b) % news), device_id_type=MESH)
    around[0] = pay_ref[...]
    pl.semaphore_wait(barrier, len(greeted))
    copies = []
    for n, (a, b) in enumerate(column):
        copy = pltpu.make_async_remote_copy(
            src_ref=pay_ref,
            dst_ref=around.at[olds - a],
            send_sem=send_sem.at[n],
            recv_sem=recv_sem.at[n],
            device_id=((i + a) % olds, (j + b) % news),
            device_id_type=MESH,
        )
        copy.start()
        copies.append(copy)
    for n, (a, b) in enumerate(sides):
        side = 1 if b == 1 else 0
        copy = pltpu.make_async_remote_copy(
            src_ref=edge_ref.at[side],
            dst_ref=edges.at[side, (olds - a) % olds],
            send_sem=edge_send.at[n],
            recv_sem=edge_recv.at[n],
            device_id=((i + a) % olds, (j + b) % news),
            device_id_type=MESH,
        )
        copy.start()
        copies.append(copy)
    for copy in copies:
        copy.wait()

    group = edge_ref.shape[1]
    lane = lax.broadcasted_iota(jnp.int32, (1, 1, cz), 2)
    after = jnp.concatenate([edges[0, a] for a in range(olds)], axis=1)
    before = jnp.concatenate([edges[1, a] for a in range(olds)], axis=1)
    for t in range(cz // EDGE):
        first = pltpu.roll(after, (cz - EDGE * t) % cz, 2)
        last = pltpu.roll(before, (2 * cz - EDGE - EDGE * t) % cz, 2)
        ghost[t * group : (t + 1) * group] = jnp.where(lane < EDGE, first, jnp.where(lane >= cz - EDGE, last, 0.0))

    def joined(first, count):
        rows = pl.ds(first, count)
        mine = jnp.concatenate([around[a, rows] for a in range(olds)], axis=1)
        return jnp.concatenate([mine, ghost[rows]], axis=2)

    def up_y(v):
        return pltpu.roll(v, 1, v.ndim - 2)

    def up_z(v):
        return pltpu.roll(v, 1, v.ndim - 1)

    def down_y(v):
        return pltpu.roll(v, v.shape[-2] - 1, v.ndim - 2)

    def down_z(v):
        return pltpu.roll(v, v.shape[-1] - 1, v.ndim - 1)

    volume[...] = joined(volume_at, cx) * (1.0 / 3375.0)

    def assemble(big_x, carry):
        part = [[joined(row_of(big_x, a2, a3, 0), 3) for a3 in range(3)] for a2 in range(3)]
        flat = [[part[a2][0] + up_z(part[a2][2]), part[a2][1]] for a2 in range(3)]
        for q in range(2):
            b0[q, big_x] = flat[0][q] + up_y(flat[2][q])
            b0[2 + q, big_x] = flat[1][q]
        return carry

    lax.fori_loop(0, nodes_x, assemble, 0)

    def mass(source, target):
        def component(c, carry):
            gathered = {}

            def node(big_x, a2, a3):
                v = source[(a2 % 2) * 2 + a3 % 2, big_x, c]
                if a2 == 2:
                    v = down_y(v)
                if a3 == 2:
                    v = down_z(v)
                return v

            for big_x in range(nodes_x):
                grid = [[node(big_x, a2, a3) for a3 in range(3)] for a2 in range(3)]
                grid = [line(*grid[a2]) for a2 in range(3)]
                grid = list(zip(*[line(grid[0][a3], grid[1][a3], grid[2][a3]) for a3 in range(3)]))
                gathered[big_x] = grid
            out = {}
            for a2 in range(3):
                for a3 in range(3):
                    for x in range(cx):
                        ends = line(*[gathered[2 * x + a1][a2][a3] for a1 in range(3)])
                        for a1 in range(3):
                            term = ends[a1] * volume[x]
                            key = (2 * x + a1, a2, a3)
                            out[key] = out[key] + term if key in out else term
            for big_x in range(nodes_x):
                flat = [[out[big_x, a2, 0] + up_z(out[big_x, a2, 2]), out[big_x, a2, 1]] for a2 in range(3)]
                for q in range(2):
                    target[q, big_x, c] = flat[0][q] + up_y(flat[2][q])
                    target[2 + q, big_x, c] = flat[1][q]
            return carry

        lax.fori_loop(0, 3, component, 0)

    def products(turn, pairs):
        held = sorted({n for pair in pairs for n in pair})
        buffers = (b0, b1, b2, b3, b4)
        parts[turn] = jnp.zeros(parts.shape[1:], F32)
        for c in range(3):
            totals = [jnp.zeros((ny, cz), F32) for _ in pairs]
            for q in range(4):
                for big_x in range(nodes_x):
                    v = {n: buffers[n][q, big_x, c, :, :cz] for n in held}
                    totals = [t + v[m] * v[n] for t, (m, n) in zip(totals, pairs)]
            for n, t in enumerate(totals):
                row = 3 * n + c
                parts[turn, row : row + 1, :] = jnp.sum(t, axis=0, keepdims=True)
        copies = []
        for n, (a, b) in enumerate(ring):
            copy = pltpu.make_async_remote_copy(
                src_ref=parts.at[turn],
                dst_ref=sums.at[turn, j],
                send_sem=sum_send.at[turn, n],
                recv_sem=sum_recv.at[turn, n],
                device_id=(i, (j + b) % news),
                device_id_type=MESH,
            )
            copy.start()
            copies.append(copy)
        sums[turn, j] = parts[turn]
        for copy in copies:
            copy.wait()
        whole = sums[turn, 0]
        for b in range(1, news):
            whole = whole + sums[turn, b]
        whole = jnp.sum(whole, axis=1, keepdims=True)
        return [whole[3 * n : 3 * n + 3] for n in range(len(pairs))]

    every = [(q, big_x) for q in range(4) for big_x in range(nodes_x)]

    mass(b0, b1)
    mass(b1, b2)
    g00, g01, g11, g12, g22 = products(0, [(0, 0), (0, 1), (1, 1), (1, 2), (2, 2)])
    step0 = g00 / g01
    norm1 = g00 - 2.0 * step0 * g01 + step0 * step0 * g11
    share0 = 1.0 + norm1 / g00
    step1 = norm1 / (share0 * share0 * g01 - 2.0 * share0 * step0 * g11 + step0 * step0 * g12)
    e1, e2 = step0 + step1 * share0, step0 * step1
    norm2 = (g00 - 2.0 * e1 * g01 + (e1 * e1 + 2.0 * e2) * g11 - 2.0 * e1 * e2 * g12 + e2 * e2 * g22)
    share1 = norm2 / norm1
    for c in range(3):
        s = [v[c : c + 1] for v in (step0, step1, share0, share1, e1, e2)]
        for q, big_x in every:
            at = (q, big_x, c)
            r, m1 = b0[at], b1[at]
            way = s[2] * r - s[0] * m1
            ans[at] = s[0] * r[:, :cz] + s[1] * way[:, :cz]
            r = r - s[4] * m1 + s[5] * b2[at]
            b0[at] = r
            b1[at] = r + s[3] * way
    mass(b1, b2)
    mass(b2, b3)
    mass(b0, b4)
    rr, pm, rm, mm, rmr, mmm, rmm = products(1, [(0, 0), (1, 2), (0, 2), (2, 2), (0, 4), (2, 3), (0, 3)])
    step2 = rr / pm
    norm3 = rr - 2.0 * step2 * rm + step2 * step2 * mm
    share2 = norm3 / rr
    curve = (rmr + step2 * step2 * mmm + share2 * share2 * pm - 2.0 * step2 * rmm + 2.0 * share2 * rm
             - 2.0 * step2 * share2 * mm)
    step3 = norm3 / curve
    for c in range(3):
        s2, s3, h2 = (v[c : c + 1] for v in (step2, step3, share2))
        for q, big_x in every:
            at = (q, big_x, c, slice(None), slice(0, cz))
            p, m = b1[at], b2[at]
            r = b0[at] - s2 * m
            way = r + h2 * p
            ans[q, big_x, c] = ans[q, big_x, c] + s2 * p + s3 * way
            b0[at] = r - s3 * (b4[at] - s2 * b3[at] + h2 * m)

    span = 2 * cy
    for o, source in enumerate((ans, b0)):
        for c in range(3):
            for q, big_x in every:
                for y in range(cy):
                    row = ((o * 3 + c) * nodes_x + big_x) * span + 2 * y + q // 2
                    z = (q % 2) * cz
                    woven[row : row + 1, z : z + cz] = source[q, big_x, c, y : y + 1, :cz]
    lines = lax.broadcasted_iota(jnp.int32, (2 * cz, 2 * cz), 0)
    columns = lax.broadcasted_iota(jnp.int32, (2 * cz, 2 * cz), 1)
    spot = jnp.where(lines < cz, 2 * lines, 2 * (lines - cz) + 1)
    weave = jnp.where(spot == columns, 1.0, 0.0)
    result = jnp.dot(woven[...], weave, precision=lax.Precision.HIGHEST, preferred_element_type=F32)
    for o, target in enumerate((sol_ref, res_ref)):
        for c in range(3):
            for big_x in range(nodes_x):
                row = ((o * 3 + c) * nodes_x + big_x) * span
                target[c, big_x] = result[row : row + span]


def on_device(olds, news, old_field, pair_dest, pair_new, pair_old, pair_block, basis_old, basis_new, volume):
    devices = olds * news
    pairs = pair_dest.shape[0]
    cap = 4 * pairs // devices
    cells = volume.shape
    elements = math.prod(cells)
    smem = pl.BlockSpec(memory_space=pltpu.SMEM)
    vmem = pl.BlockSpec(memory_space=VMEM)
    outgoing = pl.pallas_call(
        functools.partial(pack_kernel, devices, cap),
        out_shape=jax.ShapeDtypeStruct((devices, ROWS, cap), BF16),
        in_specs=[smem] * 4 + [vmem],
        out_specs=vmem,
        scratch_shapes=[
            VMEM((128, 128), F32),
            VMEM((old_field.shape[2], 128), F32),
            VMEM((devices * cap, 128), F32),
            pltpu.SMEM((devices,), jnp.int32),
        ],
        name="pack",
    )(pair_dest.reshape(-1), pair_new, pair_old, pair_block, old_field)
    arrived = pl.pallas_call(
        functools.partial(exchange_kernel, olds, news, cap),
        out_shape=jax.ShapeDtypeStruct((ROWS, devices * cap), BF16),
        in_specs=[vmem],
        out_specs=vmem,
        scratch_shapes=[
            pltpu.SemaphoreType.DMA((devices,)),
            pltpu.SemaphoreType.DMA((devices,)),
            pltpu.SemaphoreType.DMA,
        ],
        compiler_params=pltpu.CompilerParams(collective_id=0, has_side_effects=True),
        name="exchange",
    )(outgoing)
    kinds = basis_old.shape[0]
    wide = 128 * pl.cdiv(basis_old.shape[2], 128)
    chunk = 4 * 128
    cz = cells[2]
    groups = cz // EDGE
    group = pl.cdiv(row_of(2 * cells[0] + 1, 0, 0, 0) + cells[0], groups)
    pay_rows = groups * group
    payload, edge = pl.pallas_call(
        functools.partial(load_kernel, cells, chunk),
        out_shape=(
            jax.ShapeDtypeStruct((pay_rows,) + cells[1:], F32),
            jax.ShapeDtypeStruct((2, group) + cells[1:], F32),
        ),
        in_specs=[vmem] * 4,
        out_specs=(vmem, vmem),
        scratch_shapes=[
            VMEM((kinds * ROWS, 3 * wide), F32),
            VMEM((3 * wide, kinds * ROWS), BF16),
            VMEM((kinds * ROWS, 3 * wide), BF16),
            VMEM((2 * ROWS, elements), F32),
            VMEM((ROWS, elements), F32),
        ],
        name="load",
    )(arrived, jnp.transpose(basis_old, (1, 0, 2)), jnp.transpose(basis_new, (1, 0, 2)), volume)
    nodes_x = 2 * cells[0] + 1
    ny = olds * cells[1]
    grid = (4, nodes_x, 3)
    own = jax.ShapeDtypeStruct((3, nodes_x, 2 * cells[1], 2 * cz), F32)
    return pl.pallas_call(
        functools.partial(solve_kernel, olds, news, cells),
        out_shape=(own, own),
        in_specs=[vmem, vmem],
        out_specs=(vmem, vmem),
        scratch_shapes=[
            VMEM((olds, pay_rows) + cells[1:], F32),
            VMEM((2, olds, group) + cells[1:], F32),
            VMEM((pay_rows, ny, cz), F32),
            VMEM((cells[0], ny, 2 * cz), F32),
        ]
        + [VMEM(grid + (ny, 2 * cz), F32)] * 5
        + [
            VMEM(grid + (ny, cz), F32),
            VMEM((2, 24, cz), F32),
            VMEM((2, news, 24, cz), F32),
            VMEM((2 * 3 * nodes_x * 2 * cells[1], 2 * cz), F32),
            pltpu.SemaphoreType.DMA((olds,)),
            pltpu.SemaphoreType.DMA((olds,)),
            pltpu.SemaphoreType.DMA((2 * olds,)),
            pltpu.SemaphoreType.DMA((2 * olds,)),
            pltpu.SemaphoreType.DMA((2, news)),
            pltpu.SemaphoreType.DMA((2, news)),
        ],
        compiler_params=pltpu.CompilerParams(collective_id=1, has_side_effects=True),
        name="solve",
    )(payload, edge)


def solution(mesh):
    in_specs = (
        P(None, None, ("old", "new")),
        P(("old", "new"), None),
        P(("old", "new")),
        P(("old", "new")),
        P(("old", "new")),
        P(),
        P(),
        P(None, "old", "new"),
    )
    out_specs = (P(None, None, "old", "new"), P(None, None, "old", "new"))
    return jax.shard_map(
        functools.partial(on_device, mesh.shape["old"], mesh.shape["new"]),
        mesh=mesh,
        in_specs=in_specs,
        out_specs=out_specs,
        check_vma=False,
    )
```

```python
import functools
import math

import jax
import jax.numpy as jnp
from jax import lax
from jax.experimental import pallas as pl
from jax.experimental.pallas import tpu as pltpu
from jax.sharding import PartitionSpec as P

MESH = pl.DeviceIdType.MESH
VMEM = pltpu.VMEM
STRIDE = 32
ROWS = 3 * STRIDE
EDGE = 8
KINDS_AT = 27
F32 = jnp.float32
BF16 = jnp.bfloat16


def pack_kernel(devices, cap, dest_ref, new_ref, old_idx_ref, block_ref, field_ref, out_ref, square, rows, slots, count):
    lanes = rows.shape[1]
    old_elements = field_ref.shape[2]
    for c in range(3):
        square[c * STRIDE : c * STRIDE + 27, :] = field_ref[c].astype(F32)
        square[c * STRIDE + 27 : (c + 1) * STRIDE, :] = jnp.zeros((STRIDE - 27, old_elements), F32)
    square[ROWS:, :] = jnp.zeros((lanes - ROWS, old_elements), F32)

    def turn(j, carry):
        at = pl.ds(pl.multiple_of(j * lanes, lanes), lanes)
        rows[at, :] = square[:, at].T
        return carry

    lax.fori_loop(0, old_elements // lanes, turn, 0, unroll=4)
    slots[...] = jnp.zeros_like(slots)

    def clear(d, carry):
        count[d] = 0
        return carry

    lax.fori_loop(0, devices, clear, 0)
    lane = lax.broadcasted_iota(jnp.int32, (1, lanes), 1)

    def place(p, carry):
        d = dest_ref[p]
        rank = count[d]
        count[d] = rank + 1
        code = (new_ref[p] * 4 + block_ref[p]).astype(F32)
        row = rows[pl.ds(old_idx_ref[p], 1), :]
        slots[pl.ds(d * cap + rank, 1), :] = jnp.where(lane == KINDS_AT, code, row)
        return carry

    lax.fori_loop(0, dest_ref.shape[0], place, 0, unroll=8)

    row_at = lax.broadcasted_iota(jnp.int32, (ROWS, cap), 0)

    def send_form(d, carry):
        block = slots[pl.ds(pl.multiple_of(d * cap, cap), cap), :].T[:ROWS]
        code = block[KINDS_AT : KINDS_AT + 1].astype(jnp.int32)
        high = (code // 512).astype(F32)
        low = ((code // 4) % 128).astype(F32)
        kind = (code % 4).astype(F32)
        block = jnp.where(row_at == KINDS_AT, high, block)
        block = jnp.where(row_at == KINDS_AT + 1, low, block)
        block = jnp.where(row_at == KINDS_AT + 2, kind, block)
        out_ref[d] = block.astype(BF16)
        return carry

    lax.fori_loop(0, devices, send_form, 0, unroll=4)


def row_of(big_x, a2, a3, c):
    return ((big_x * 3 + a2) * 3 + a3) * 3 + c


def load_kernel(olds, news, cells, cap, together, out_ref, old_ref, new_ref, volume_ref, pay_ref, edge_ref, in_ref, square,
                first, second, total, load, send_sem, recv_sem):
    i, j = lax.axis_index("old"), lax.axis_index("new")
    peers = sorted(((a, b) for a in range(olds) for b in range(news) if a or b), key=lambda p: (abs(p[1] - news // 2), p))
    place = {peer: n for n, peer in enumerate(peers + [(0, 0)])}
    barrier = pltpu.get_barrier_semaphore()
    for a, b in peers:
        pl.semaphore_signal(barrier, inc=1, device_id=((i + a) % olds, (j + b) % news), device_id_type=MESH)
    n = place[0, 0]
    pltpu.make_async_copy(out_ref.at[i * news + j], in_ref.at[:, n * cap : (n + 1) * cap], recv_sem.at[n]).start()
    pl.semaphore_wait(barrier, len(peers))
    copies = []
    for a, b in peers:
        target = ((i + a) % olds, (j + b) % news)
        n = place[(olds - a) % olds, (news - b) % news]
        copy = pltpu.make_async_remote_copy(
            src_ref=out_ref.at[target[0] * news + target[1]],
            dst_ref=in_ref.at[:, n * cap : (n + 1) * cap],
            send_sem=send_sem.at[n],
            recv_sem=recv_sem.at[n],
            device_id=target,
            device_id_type=MESH,
        )
        copy.start()
        copies.append(copy)
    chunk = together * cap
    _, kinds, points = old_ref.shape
    wide = square.shape[1] // 3
    elements = cells[0] * cells[1] * cells[2]
    for source in (old_ref, new_ref):
        square[...] = jnp.zeros_like(square)
        for q in range(kinds):
            for c in range(3):
                at = q * ROWS + c * STRIDE
                square[at : at + 27, c * wide : c * wide + points] = source[:, q].astype(F32)
        if source is old_ref:
            first[...] = square[...].T.astype(BF16)
        else:
            second[...] = square[...].astype(BF16)
    total[...] = jnp.zeros_like(total)

    def step(s, carry):
        for n in range(together):
            spot = pl.ds(pl.multiple_of(s * chunk + n * cap, cap), cap)
            pltpu.make_async_copy(out_ref.at[0], in_ref.at[:, spot], recv_sem.at[s * together + n]).wait()
        at = pl.ds(pl.multiple_of(s * chunk, chunk), chunk)
        block = in_ref[:, at].astype(F32)
        kind = block[KINDS_AT + 2 : KINDS_AT + 3]
        element = (block[KINDS_AT : KINDS_AT + 1] * 128.0 + block[KINDS_AT + 1 : KINDS_AT + 2]).astype(jnp.int32)
        chosen = jnp.concatenate([jnp.where(kind == q, block, 0.0) for q in range(kinds)], axis=0).astype(BF16)
        values = jnp.dot(first[...], chosen, preferred_element_type=F32).astype(BF16)
        every = jnp.dot(second[...], values, preferred_element_type=F32)
        part = jnp.zeros((ROWS, chunk), F32)
        for q in range(kinds):
            part = part + jnp.where(kind == q, every[q * ROWS : (q + 1) * ROWS], 0.0)
        high = part.astype(BF16)
        low = (part - high.astype(F32)).astype(BF16)
        onehot = jnp.where(
            lax.broadcasted_iota(jnp.int32, (elements, chunk), 0) == element, 1.0, 0.0
        ).astype(BF16)
        total[...] += lax.dot_general(
            jnp.concatenate([high, low], axis=0), onehot, (((1,), (1,)), ((), ())), preferred_element_type=F32
        )
        return carry

    lax.fori_loop(0, in_ref.shape[1] // chunk, step, 0)
    load[...] = total[:ROWS] + total[ROWS:]
    for big_x in range(2 * cells[0] + 1):
        for a2 in range(3):
            for a3 in range(3):
                for c in range(3):
                    for y in range(cells[1]):
                        value = None
                        for x in range(cells[0]):
                            a1 = big_x - 2 * x
                            if 0 <= a1 <= 2:
                                r = c * STRIDE + a1 * 9 + a2 * 3 + a3
                                z = (x * cells[1] + y) * cells[2]
                                term = load[r : r + 1, z : z + cells[2]]
                                value = term if value is None else value + term
                        pay_ref[row_of(big_x, a2, a3, c), y : y + 1, :] = value
    for x in range(cells[0]):
        pay_ref[row_of(2 * cells[0] + 1, 0, 0, 0) + x] = volume_ref[x]
    group, cz = edge_ref.shape[1], cells[2]
    for r in range(row_of(2 * cells[0] + 1, 0, 0, 0) + cells[0], pay_ref.shape[0]):
        pay_ref[r] = jnp.zeros(cells[1:], F32)
    lane = lax.broadcasted_iota(jnp.int32, (1, 1, cz), 2)
    first_cells = jnp.zeros(edge_ref.shape[1:], F32)
    last_cells = jnp.zeros(edge_ref.shape[1:], F32)
    for t in range(cz // EDGE):
        rows = pay_ref[t * group : (t + 1) * group]
        here = lane // EDGE == t
        first_cells = jnp.where(here, pltpu.roll(rows, EDGE * t, 2), first_cells)
        last_cells = jnp.where(here, pltpu.roll(rows, (EDGE * t + EDGE) % cz, 2), last_cells)
    edge_ref[0] = first_cells
    edge_ref[1] = last_cells
    for copy in copies:
        copy.wait_send()


def line(a, b, c):
    ends = 2.0 * b
    return 4.0 * a + ends - c, 2.0 * (a + c) + 16.0 * b, 4.0 * c + ends - a


def solve_kernel(olds, news, cells, pay_ref, edge_ref, sol_ref, res_ref, around, edges, ghost, volume, b0, b1, b2, b3, b4,
                 ans, parts, sums, woven, send_sem, recv_sem, edge_send, edge_recv, sum_send, sum_recv):
    i, j = lax.axis_index("old"), lax.axis_index("new")
    cx, cy, cz = cells
    nodes_x = 2 * cx + 1
    ny = olds * cy
    volume_at = row_of(nodes_x, 0, 0, 0)
    column = [(a, 0) for a in range(1, olds)]
    sides = [(a, b) for b in (1, news - 1) for a in range(olds)]
    ring = [(0, b) for b in range(1, news)]
    barrier = pltpu.get_barrier_semaphore()
    greeted = column + sides + [peer for peer in ring if peer not in sides]
    for a, b in greeted:
        pl.semaphore_signal(barrier, inc=1, device_id=((i + a) % olds, (j + b) % news), device_id_type=MESH)
    around[0] = pay_ref[...]
    pl.semaphore_wait(barrier, len(greeted))
    copies = []
    for n, (a, b) in enumerate(column):
        copy = pltpu.make_async_remote_copy(
            src_ref=pay_ref,
            dst_ref=around.at[olds - a],
            send_sem=send_sem.at[n],
            recv_sem=recv_sem.at[n],
            device_id=((i + a) % olds, (j + b) % news),
            device_id_type=MESH,
        )
        copy.start()
        copies.append(copy)
    for n, (a, b) in enumerate(sides):
        side = 1 if b == 1 else 0
        copy = pltpu.make_async_remote_copy(
            src_ref=edge_ref.at[side],
            dst_ref=edges.at[side, (olds - a) % olds],
            send_sem=edge_send.at[n],
            recv_sem=edge_recv.at[n],
            device_id=((i + a) % olds, (j + b) % news),
            device_id_type=MESH,
        )
        copy.start()
        copies.append(copy)
    for copy in copies:
        copy.wait()

    group = edge_ref.shape[1]
    lane = lax.broadcasted_iota(jnp.int32, (1, 1, cz), 2)
    after = jnp.concatenate([edges[0, a] for a in range(olds)], axis=1)
    before = jnp.concatenate([edges[1, a] for a in range(olds)], axis=1)
    for t in range(cz // EDGE):
        first = pltpu.roll(after, (cz - EDGE * t) % cz, 2)
        last = pltpu.roll(before, (2 * cz - EDGE - EDGE * t) % cz, 2)
        ghost[t * group : (t + 1) * group] = jnp.where(lane < EDGE, first, jnp.where(lane >= cz - EDGE, last, 0.0))

    def joined(first, count):
        rows = pl.ds(first, count)
        mine = jnp.concatenate([around[a, rows] for a in range(olds)], axis=1)
        return jnp.concatenate([mine, ghost[rows]], axis=2)

    def up_y(v):
        return pltpu.roll(v, 1, v.ndim - 2)

    def up_z(v):
        return pltpu.roll(v, 1, v.ndim - 1)

    def down_y(v):
        return pltpu.roll(v, v.shape[-2] - 1, v.ndim - 2)

    def down_z(v):
        return pltpu.roll(v, v.shape[-1] - 1, v.ndim - 1)

    volume[...] = joined(volume_at, cx) * (1.0 / 3375.0)

    def assemble(big_x, carry):
        part = [[joined(row_of(big_x, a2, a3, 0), 3) for a3 in range(3)] for a2 in range(3)]
        flat = [[part[a2][0] + up_z(part[a2][2]), part[a2][1]] for a2 in range(3)]
        for q in range(2):
            b0[q, big_x] = flat[0][q] + up_y(flat[2][q])
            b0[2 + q, big_x] = flat[1][q]
        return carry

    lax.fori_loop(0, nodes_x, assemble, 0)

    def mass(source, target):
        def component(c, carry):
            gathered = {}

            def node(big_x, a2, a3):
                v = source[(a2 % 2) * 2 + a3 % 2, big_x, c]
                if a2 == 2:
                    v = down_y(v)
                if a3 == 2:
                    v = down_z(v)
                return v

            for big_x in range(nodes_x):
                grid = [[node(big_x, a2, a3) for a3 in range(3)] for a2 in range(3)]
                grid = [line(*grid[a2]) for a2 in range(3)]
                grid = list(zip(*[line(grid[0][a3], grid[1][a3], grid[2][a3]) for a3 in range(3)]))
                gathered[big_x] = grid
            out = {}
            for a2 in range(3):
                for a3 in range(3):
                    for x in range(cx):
                        ends = line(*[gathered[2 * x + a1][a2][a3] for a1 in range(3)])
                        for a1 in range(3):
                            term = ends[a1] * volume[x]
                            key = (2 * x + a1, a2, a3)
                            out[key] = out[key] + term if key in out else term
            for big_x in range(nodes_x):
                flat = [[out[big_x, a2, 0] + up_z(out[big_x, a2, 2]), out[big_x, a2, 1]] for a2 in range(3)]
                for q in range(2):
                    target[q, big_x, c] = flat[0][q] + up_y(flat[2][q])
                    target[2 + q, big_x, c] = flat[1][q]
            return carry

        lax.fori_loop(0, 3, component, 0)

    def products(turn, pairs):
        held = sorted({n for pair in pairs for n in pair})
        buffers = (b0, b1, b2, b3, b4)
        parts[turn] = jnp.zeros(parts.shape[1:], F32)
        for c in range(3):
            totals = [jnp.zeros((ny, cz), F32) for _ in pairs]
            for q in range(4):
                for big_x in range(nodes_x):
                    v = {n: buffers[n][q, big_x, c, :, :cz] for n in held}
                    totals = [t + v[m] * v[n] for t, (m, n) in zip(totals, pairs)]
            for n, t in enumerate(totals):
                row = 3 * n + c
                parts[turn, row : row + 1, :] = jnp.sum(t, axis=0, keepdims=True)
        copies = []
        for n, (a, b) in enumerate(ring):
            copy = pltpu.make_async_remote_copy(
                src_ref=parts.at[turn],
                dst_ref=sums.at[turn, j],
                send_sem=sum_send.at[turn, n],
                recv_sem=sum_recv.at[turn, n],
                device_id=(i, (j + b) % news),
                device_id_type=MESH,
            )
            copy.start()
            copies.append(copy)
        sums[turn, j] = parts[turn]
        for copy in copies:
            copy.wait()
        whole = sums[turn, 0]
        for b in range(1, news):
            whole = whole + sums[turn, b]
        whole = jnp.sum(whole, axis=1, keepdims=True)
        return [whole[3 * n : 3 * n + 3] for n in range(len(pairs))]

    every = [(q, big_x) for q in range(4) for big_x in range(nodes_x)]

    mass(b0, b1)
    mass(b1, b2)
    g00, g01, g11, g12, g22 = products(0, [(0, 0), (0, 1), (1, 1), (1, 2), (2, 2)])
    step0 = g00 / g01
    norm1 = g00 - 2.0 * step0 * g01 + step0 * step0 * g11
    share0 = 1.0 + norm1 / g00
    step1 = norm1 / (share0 * share0 * g01 - 2.0 * share0 * step0 * g11 + step0 * step0 * g12)
    e1, e2 = step0 + step1 * share0, step0 * step1
    norm2 = (g00 - 2.0 * e1 * g01 + (e1 * e1 + 2.0 * e2) * g11 - 2.0 * e1 * e2 * g12 + e2 * e2 * g22)
    share1 = norm2 / norm1
    for c in range(3):
        s = [v[c : c + 1] for v in (step0, step1, share0, share1, e1, e2)]
        for q, big_x in every:
            at = (q, big_x, c)
            r, m1 = b0[at], b1[at]
            way = s[2] * r - s[0] * m1
            ans[at] = s[0] * r[:, :cz] + s[1] * way[:, :cz]
            r = r - s[4] * m1 + s[5] * b2[at]
            b0[at] = r
            b1[at] = r + s[3] * way
    mass(b1, b2)
    mass(b2, b3)
    mass(b0, b4)
    rr, pm, rm, mm, rmr, mmm, rmm = products(1, [(0, 0), (1, 2), (0, 2), (2, 2), (0, 4), (2, 3), (0, 3)])
    step2 = rr / pm
    norm3 = rr - 2.0 * step2 * rm + step2 * step2 * mm
    share2 = norm3 / rr
    curve = (rmr + step2 * step2 * mmm + share2 * share2 * pm - 2.0 * step2 * rmm + 2.0 * share2 * rm
             - 2.0 * step2 * share2 * mm)
    step3 = norm3 / curve
    for c in range(3):
        s2, s3, h2 = (v[c : c + 1] for v in (step2, step3, share2))
        for q, big_x in every:
            at = (q, big_x, c, slice(None), slice(0, cz))
            p, m = b1[at], b2[at]
            r = b0[at] - s2 * m
            way = r + h2 * p
            ans[q, big_x, c] = ans[q, big_x, c] + s2 * p + s3 * way
            b0[at] = r - s3 * (b4[at] - s2 * b3[at] + h2 * m)

    span = 2 * cy
    for o, source in enumerate((ans, b0)):
        for c in range(3):
            for q, big_x in every:
                for y in range(cy):
                    row = ((o * 3 + c) * nodes_x + big_x) * span + 2 * y + q // 2
                    z = (q % 2) * cz
                    woven[row : row + 1, z : z + cz] = source[q, big_x, c, y : y + 1, :cz]
    lines = lax.broadcasted_iota(jnp.int32, (2 * cz, 2 * cz), 0)
    columns = lax.broadcasted_iota(jnp.int32, (2 * cz, 2 * cz), 1)
    spot = jnp.where(lines < cz, 2 * lines, 2 * (lines - cz) + 1)
    weave = jnp.where(spot == columns, 1.0, 0.0)
    result = jnp.dot(woven[...], weave, precision=lax.Precision.HIGHEST, preferred_element_type=F32)
    for o, target in enumerate((sol_ref, res_ref)):
        for c in range(3):
            for big_x in range(nodes_x):
                row = ((o * 3 + c) * nodes_x + big_x) * span
                target[c, big_x] = result[row : row + span]


def on_device(olds, news, old_field, pair_dest, pair_new, pair_old, pair_block, basis_old, basis_new, volume):
    devices = olds * news
    pairs = pair_dest.shape[0]
    cap = 4 * pairs // devices
    cells = volume.shape
    elements = math.prod(cells)
    smem = pl.BlockSpec(memory_space=pltpu.SMEM)
    vmem = pl.BlockSpec(memory_space=VMEM)
    outgoing = pl.pallas_call(
        functools.partial(pack_kernel, devices, cap),
        out_shape=jax.ShapeDtypeStruct((devices, ROWS, cap), BF16),
        in_specs=[smem] * 4 + [vmem],
        out_specs=vmem,
        scratch_shapes=[
            VMEM((128, old_field.shape[2]), F32),
            VMEM((old_field.shape[2], 128), F32),
            VMEM((devices * cap, 128), F32),
            pltpu.SMEM((devices,), jnp.int32),
        ],
        name="pack",
    )(pair_dest.reshape(-1), pair_new, pair_old, pair_block, old_field)
    kinds = basis_old.shape[0]
    wide = 128 * pl.cdiv(basis_old.shape[2], 128)
    together = 4
    cz = cells[2]
    groups = cz // EDGE
    group = pl.cdiv(row_of(2 * cells[0] + 1, 0, 0, 0) + cells[0], groups)
    pay_rows = groups * group
    payload, edge = pl.pallas_call(
        functools.partial(load_kernel, olds, news, cells, cap, together),
        out_shape=(
            jax.ShapeDtypeStruct((pay_rows,) + cells[1:], F32),
            jax.ShapeDtypeStruct((2, group) + cells[1:], F32),
        ),
        in_specs=[vmem] * 4,
        out_specs=(vmem, vmem),
        scratch_shapes=[
            VMEM((ROWS, devices * cap), BF16),
            VMEM((kinds * ROWS, 3 * wide), F32),
            VMEM((3 * wide, kinds * ROWS), BF16),
            VMEM((kinds * ROWS, 3 * wide), BF16),
            VMEM((2 * ROWS, elements), F32),
            VMEM((ROWS, elements), F32),
            pltpu.SemaphoreType.DMA((devices,)),
            pltpu.SemaphoreType.DMA((devices,)),
        ],
        compiler_params=pltpu.CompilerParams(collective_id=0, has_side_effects=True),
        name="load",
    )(outgoing, jnp.transpose(basis_old, (1, 0, 2)), jnp.transpose(basis_new, (1, 0, 2)), volume)
    nodes_x = 2 * cells[0] + 1
    ny = olds * cells[1]
    grid = (4, nodes_x, 3)
    own = jax.ShapeDtypeStruct((3, nodes_x, 2 * cells[1], 2 * cz), F32)
    return pl.pallas_call(
        functools.partial(solve_kernel, olds, news, cells),
        out_shape=(own, own),
        in_specs=[vmem, vmem],
        out_specs=(vmem, vmem),
        scratch_shapes=[
            VMEM((olds, pay_rows) + cells[1:], F32),
            VMEM((2, olds, group) + cells[1:], F32),
            VMEM((pay_rows, ny, cz), F32),
            VMEM((cells[0], ny, 2 * cz), F32),
        ]
        + [VMEM(grid + (ny, 2 * cz), F32)] * 5
        + [
            VMEM(grid + (ny, cz), F32),
            VMEM((2, 24, cz), F32),
            VMEM((2, news, 24, cz), F32),
            VMEM((2 * 3 * nodes_x * 2 * cells[1], 2 * cz), F32),
            pltpu.SemaphoreType.DMA((olds,)),
            pltpu.SemaphoreType.DMA((olds,)),
            pltpu.SemaphoreType.DMA((2 * olds,)),
            pltpu.SemaphoreType.DMA((2 * olds,)),
            pltpu.SemaphoreType.DMA((2, news)),
            pltpu.SemaphoreType.DMA((2, news)),
        ],
        compiler_params=pltpu.CompilerParams(collective_id=1, has_side_effects=True),
        name="solve",
    )(payload, edge)


def solution(mesh):
    in_specs = (
        P(None, None, ("old", "new")),
        P(("old", "new"), None),
        P(("old", "new")),
        P(("old", "new")),
        P(("old", "new")),
        P(),
        P(),
        P(None, "old", "new"),
    )
    out_specs = (P(None, None, "old", "new"), P(None, None, "old", "new"))
    return jax.shard_map(
        functools.partial(on_device, mesh.shape["old"], mesh.shape["new"]),
        mesh=mesh,
        in_specs=in_specs,
        out_specs=out_specs,
        check_vma=False,
    )
```

```python
import functools
import math

import jax
import jax.numpy as jnp
from jax import lax
from jax.experimental import pallas as pl
from jax.experimental.pallas import tpu as pltpu
from jax.sharding import PartitionSpec as P

MESH = pl.DeviceIdType.MESH
VMEM = pltpu.VMEM
STRIDE = 32
ROWS = 3 * STRIDE
EDGE = 8
KINDS_AT = 27
F32 = jnp.float32
BF16 = jnp.bfloat16


def pack_kernel(devices, cap, dest_ref, new_ref, old_idx_ref, block_ref, field_ref, out_ref, square, rows, slots, count):
    lanes = rows.shape[1]
    old_elements = field_ref.shape[2]
    for c in range(3):
        square[c * STRIDE : c * STRIDE + 27, :] = field_ref[c].astype(F32)
        square[c * STRIDE + 27 : (c + 1) * STRIDE, :] = jnp.zeros((STRIDE - 27, old_elements), F32)
    square[ROWS:, :] = jnp.zeros((lanes - ROWS, old_elements), F32)

    def turn(j, carry):
        at = pl.ds(pl.multiple_of(j * lanes, lanes), lanes)
        rows[at, :] = square[:, at].T
        return carry

    lax.fori_loop(0, old_elements // lanes, turn, 0, unroll=4)
    slots[...] = jnp.zeros_like(slots)

    def clear(d, carry):
        count[d] = 0
        return carry

    lax.fori_loop(0, devices, clear, 0)
    lane = lax.broadcasted_iota(jnp.int32, (1, lanes), 1)

    def place(p, carry):
        d = dest_ref[p]
        rank = count[d]
        count[d] = rank + 1
        code = (new_ref[p] * 4 + block_ref[p]).astype(F32)
        row = rows[pl.ds(old_idx_ref[p], 1), :]
        slots[pl.ds(d * cap + rank, 1), :] = jnp.where(lane == KINDS_AT, code, row)
        return carry

    lax.fori_loop(0, dest_ref.shape[0], place, 0, unroll=16)

    row_at = lax.broadcasted_iota(jnp.int32, (ROWS, cap), 0)

    def send_form(d, carry):
        block = slots[pl.ds(pl.multiple_of(d * cap, cap), cap), :].T[:ROWS]
        code = block[KINDS_AT : KINDS_AT + 1].astype(jnp.int32)
        high = (code // 512).astype(F32)
        low = ((code // 4) % 128).astype(F32)
        kind = (code % 4).astype(F32)
        block = jnp.where(row_at == KINDS_AT, high, block)
        block = jnp.where(row_at == KINDS_AT + 1, low, block)
        block = jnp.where(row_at == KINDS_AT + 2, kind, block)
        out_ref[d] = block.astype(BF16)
        return carry

    lax.fori_loop(0, devices, send_form, 0, unroll=4)


def row_of(big_x, a2, a3, c):
    return ((big_x * 3 + a2) * 3 + a3) * 3 + c


def load_kernel(olds, news, cells, cap, together, out_ref, old_ref, new_ref, volume_ref, pay_ref, edge_ref, in_ref, square,
                first, second, total, load, send_sem, recv_sem):
    i, j = lax.axis_index("old"), lax.axis_index("new")
    peers = sorted(((a, b) for a in range(olds) for b in range(news) if a or b), key=lambda p: (abs(p[1] - news // 2), p))
    place = {peer: n for n, peer in enumerate(peers + [(0, 0)])}
    barrier = pltpu.get_barrier_semaphore()
    for a, b in peers:
        pl.semaphore_signal(barrier, inc=1, device_id=((i + a) % olds, (j + b) % news), device_id_type=MESH)
    n = place[0, 0]
    pltpu.make_async_copy(out_ref.at[i * news + j], in_ref.at[:, n * cap : (n + 1) * cap], recv_sem.at[n]).start()
    pl.semaphore_wait(barrier, len(peers))
    copies = []
    for a, b in peers:
        target = ((i + a) % olds, (j + b) % news)
        n = place[(olds - a) % olds, (news - b) % news]
        copy = pltpu.make_async_remote_copy(
            src_ref=out_ref.at[target[0] * news + target[1]],
            dst_ref=in_ref.at[:, n * cap : (n + 1) * cap],
            send_sem=send_sem.at[n],
            recv_sem=recv_sem.at[n],
            device_id=target,
            device_id_type=MESH,
        )
        copy.start()
        copies.append(copy)
    chunk = together * cap
    _, kinds, points = old_ref.shape
    wide = square.shape[1] // 3
    elements = cells[0] * cells[1] * cells[2]
    for source in (old_ref, new_ref):
        square[...] = jnp.zeros_like(square)
        for q in range(kinds):
            for c in range(3):
                at = q * ROWS + c * STRIDE
                square[at : at + 27, c * wide : c * wide + points] = source[:, q].astype(F32)
        if source is old_ref:
            first[...] = square[...].T.astype(BF16)
        else:
            second[...] = square[...].astype(BF16)
    total[...] = jnp.zeros_like(total)

    def step(s, carry):
        for n in range(together):
            spot = pl.ds(pl.multiple_of(s * chunk + n * cap, cap), cap)
            pltpu.make_async_copy(out_ref.at[0], in_ref.at[:, spot], recv_sem.at[s * together + n]).wait()
        at = pl.ds(pl.multiple_of(s * chunk, chunk), chunk)
        block = in_ref[:, at].astype(F32)
        kind = block[KINDS_AT + 2 : KINDS_AT + 3]
        element = (block[KINDS_AT : KINDS_AT + 1] * 128.0 + block[KINDS_AT + 1 : KINDS_AT + 2]).astype(jnp.int32)
        chosen = jnp.concatenate([jnp.where(kind == q, block, 0.0) for q in range(kinds)], axis=0).astype(BF16)
        values = jnp.dot(first[...], chosen, preferred_element_type=F32).astype(BF16)
        every = jnp.dot(second[...], values, preferred_element_type=F32)
        part = jnp.zeros((ROWS, chunk), F32)
        for q in range(kinds):
            part = part + jnp.where(kind == q, every[q * ROWS : (q + 1) * ROWS], 0.0)
        high = part.astype(BF16)
        low = (part - high.astype(F32)).astype(BF16)
        onehot = jnp.where(
            lax.broadcasted_iota(jnp.int32, (elements, chunk), 0) == element, 1.0, 0.0
        ).astype(BF16)
        total[...] += lax.dot_general(
            jnp.concatenate([high, low], axis=0), onehot, (((1,), (1,)), ((), ())), preferred_element_type=F32
        )
        return carry

    lax.fori_loop(0, in_ref.shape[1] // chunk, step, 0)
    load[...] = total[:ROWS] + total[ROWS:]
    for big_x in range(2 * cells[0] + 1):
        for a2 in range(3):
            for a3 in range(3):
                for c in range(3):
                    for y in range(cells[1]):
                        value = None
                        for x in range(cells[0]):
                            a1 = big_x - 2 * x
                            if 0 <= a1 <= 2:
                                r = c * STRIDE + a1 * 9 + a2 * 3 + a3
                                z = (x * cells[1] + y) * cells[2]
                                term = load[r : r + 1, z : z + cells[2]]
                                value = term if value is None else value + term
                        pay_ref[row_of(big_x, a2, a3, c), y : y + 1, :] = value
    for x in range(cells[0]):
        pay_ref[row_of(2 * cells[0] + 1, 0, 0, 0) + x] = volume_ref[x]
    group, cz = edge_ref.shape[1], cells[2]
    for r in range(row_of(2 * cells[0] + 1, 0, 0, 0) + cells[0], pay_ref.shape[0]):
        pay_ref[r] = jnp.zeros(cells[1:], F32)
    lane = lax.broadcasted_iota(jnp.int32, (1, 1, cz), 2)
    first_cells = jnp.zeros(edge_ref.shape[1:], F32)
    last_cells = jnp.zeros(edge_ref.shape[1:], F32)
    for t in range(cz // EDGE):
        rows = pay_ref[t * group : (t + 1) * group]
        here = lane // EDGE == t
        first_cells = jnp.where(here, pltpu.roll(rows, EDGE * t, 2), first_cells)
        last_cells = jnp.where(here, pltpu.roll(rows, (EDGE * t + EDGE) % cz, 2), last_cells)
    edge_ref[0] = first_cells
    edge_ref[1] = last_cells
    for copy in copies:
        copy.wait_send()


def line(a, b, c):
    ends = 2.0 * b
    return 4.0 * a + ends - c, 2.0 * (a + c) + 16.0 * b, 4.0 * c + ends - a


def solve_kernel(olds, news, cells, pay_ref, edge_ref, sol_ref, res_ref, around, edges, ghost, volume, b0, b1, b2, b3, b4,
                 ans, parts, sums, woven, send_sem, recv_sem, edge_send, edge_recv, sum_send, sum_recv):
    i, j = lax.axis_index("old"), lax.axis_index("new")
    cx, cy, cz = cells
    nodes_x = 2 * cx + 1
    ny = olds * cy
    volume_at = row_of(nodes_x, 0, 0, 0)
    column = [(a, 0) for a in range(1, olds)]
    sides = [(a, b) for b in (1, news - 1) for a in range(olds)]
    ring = [(0, b) for b in range(1, news)]
    barrier = pltpu.get_barrier_semaphore()
    greeted = column + sides + [peer for peer in ring if peer not in sides]
    for a, b in greeted:
        pl.semaphore_signal(barrier, inc=1, device_id=((i + a) % olds, (j + b) % news), device_id_type=MESH)
    around[0] = pay_ref[...]
    pl.semaphore_wait(barrier, len(greeted))
    copies = []

    def layers_to(source, spot, target, n):
        copy = pltpu.make_async_remote_copy(
            src_ref=source,
            dst_ref=around.at[spot],
            send_sem=send_sem.at[n],
            recv_sem=recv_sem.at[n],
            device_id=(target, j),
            device_id_type=MESH,
        )
        copy.start()
        return copy

    half = olds // 2
    partner = i + 1 - 2 * (i % 2)
    ahead = olds + 2 * (i % 2) - 1
    direct = [layers_to(pay_ref, olds - 2 * k, (i + 2 * k) % olds, k - 1) for k in range(1, half)]
    copies.append(layers_to(pay_ref, ahead % olds, partner, half - 1))
    for n, (a, b) in enumerate(sides):
        side = 1 if b == 1 else 0
        copy = pltpu.make_async_remote_copy(
            src_ref=edge_ref.at[side],
            dst_ref=edges.at[side, (olds - a) % olds],
            send_sem=edge_send.at[n],
            recv_sem=edge_recv.at[n],
            device_id=((i + a) % olds, (j + b) % news),
            device_id_type=MESH,
        )
        copy.start()
        copies.append(copy)
    for k, copy in enumerate(direct, start=1):
        copy.wait_recv()
        copies.append(layers_to(around.at[olds - 2 * k], (ahead - 2 * k) % olds, partner, half - 1 + k))
    for copy in direct:
        copy.wait_send()
    for copy in copies:
        copy.wait()

    group = edge_ref.shape[1]
    lane = lax.broadcasted_iota(jnp.int32, (1, 1, cz), 2)
    after = jnp.concatenate([edges[0, a] for a in range(olds)], axis=1)
    before = jnp.concatenate([edges[1, a] for a in range(olds)], axis=1)
    for t in range(cz // EDGE):
        first = pltpu.roll(after, (cz - EDGE * t) % cz, 2)
        last = pltpu.roll(before, (2 * cz - EDGE - EDGE * t) % cz, 2)
        ghost[t * group : (t + 1) * group] = jnp.where(lane < EDGE, first, jnp.where(lane >= cz - EDGE, last, 0.0))

    def joined(first, count):
        rows = pl.ds(first, count)
        mine = jnp.concatenate([around[a, rows] for a in range(olds)], axis=1)
        return jnp.concatenate([mine, ghost[rows]], axis=2)

    def up_y(v):
        return pltpu.roll(v, 1, v.ndim - 2)

    def up_z(v):
        return pltpu.roll(v, 1, v.ndim - 1)

    def down_y(v):
        return pltpu.roll(v, v.shape[-2] - 1, v.ndim - 2)

    def down_z(v):
        return pltpu.roll(v, v.shape[-1] - 1, v.ndim - 1)

    volume[...] = joined(volume_at, cx) * (1.0 / 3375.0)

    def assemble(big_x, carry):
        part = [[joined(row_of(big_x, a2, a3, 0), 3) for a3 in range(3)] for a2 in range(3)]
        flat = [[part[a2][0] + up_z(part[a2][2]), part[a2][1]] for a2 in range(3)]
        for q in range(2):
            b0[q, big_x] = flat[0][q] + up_y(flat[2][q])
            b0[2 + q, big_x] = flat[1][q]
        return carry

    lax.fori_loop(0, nodes_x, assemble, 0)

    def mass(source, target):
        def component(c, carry):
            gathered = {}

            def node(big_x, a2, a3):
                v = source[(a2 % 2) * 2 + a3 % 2, big_x, c]
                if a2 == 2:
                    v = down_y(v)
                if a3 == 2:
                    v = down_z(v)
                return v

            for big_x in range(nodes_x):
                grid = [[node(big_x, a2, a3) for a3 in range(3)] for a2 in range(3)]
                grid = [line(*grid[a2]) for a2 in range(3)]
                grid = list(zip(*[line(grid[0][a3], grid[1][a3], grid[2][a3]) for a3 in range(3)]))
                gathered[big_x] = grid
            out = {}
            for a2 in range(3):
                for a3 in range(3):
                    for x in range(cx):
                        ends = line(*[gathered[2 * x + a1][a2][a3] for a1 in range(3)])
                        for a1 in range(3):
                            term = ends[a1] * volume[x]
                            key = (2 * x + a1, a2, a3)
                            out[key] = out[key] + term if key in out else term
            for big_x in range(nodes_x):
                flat = [[out[big_x, a2, 0] + up_z(out[big_x, a2, 2]), out[big_x, a2, 1]] for a2 in range(3)]
                for q in range(2):
                    target[q, big_x, c] = flat[0][q] + up_y(flat[2][q])
                    target[2 + q, big_x, c] = flat[1][q]
            return carry

        lax.fori_loop(0, 3, component, 0)

    def products(turn, pairs):
        held = sorted({n for pair in pairs for n in pair})
        buffers = (b0, b1, b2, b3, b4)
        parts[turn] = jnp.zeros(parts.shape[1:], F32)
        for c in range(3):
            totals = [jnp.zeros((ny, cz), F32) for _ in pairs]
            for q in range(4):
                for big_x in range(nodes_x):
                    v = {n: buffers[n][q, big_x, c, :, :cz] for n in held}
                    totals = [t + v[m] * v[n] for t, (m, n) in zip(totals, pairs)]
            for n, t in enumerate(totals):
                row = 3 * n + c
                parts[turn, row : row + 1, :] = jnp.sum(t, axis=0, keepdims=True)
        copies = []
        for n, (a, b) in enumerate(ring):
            copy = pltpu.make_async_remote_copy(
                src_ref=parts.at[turn],
                dst_ref=sums.at[turn, j],
                send_sem=sum_send.at[turn, n],
                recv_sem=sum_recv.at[turn, n],
                device_id=(i, (j + b) % news),
                device_id_type=MESH,
            )
            copy.start()
            copies.append(copy)
        sums[turn, j] = parts[turn]
        for copy in copies:
            copy.wait()
        whole = sums[turn, 0]
        for b in range(1, news):
            whole = whole + sums[turn, b]
        whole = jnp.sum(whole, axis=1, keepdims=True)
        return [whole[3 * n : 3 * n + 3] for n in range(len(pairs))]

    every = [(q, big_x) for q in range(4) for big_x in range(nodes_x)]

    mass(b0, b1)
    mass(b1, b2)
    g00, g01, g11, g12, g22 = products(0, [(0, 0), (0, 1), (1, 1), (1, 2), (2, 2)])
    step0 = g00 / g01
    norm1 = g00 - 2.0 * step0 * g01 + step0 * step0 * g11
    share0 = 1.0 + norm1 / g00
    step1 = norm1 / (share0 * share0 * g01 - 2.0 * share0 * step0 * g11 + step0 * step0 * g12)
    e1, e2 = step0 + step1 * share0, step0 * step1
    norm2 = (g00 - 2.0 * e1 * g01 + (e1 * e1 + 2.0 * e2) * g11 - 2.0 * e1 * e2 * g12 + e2 * e2 * g22)
    share1 = norm2 / norm1
    for c in range(3):
        s = [v[c : c + 1] for v in (step0, step1, share0, share1, e1, e2)]
        for q, big_x in every:
            at = (q, big_x, c)
            r, m1 = b0[at], b1[at]
            way = s[2] * r - s[0] * m1
            ans[at] = s[0] * r[:, :cz] + s[1] * way[:, :cz]
            r = r - s[4] * m1 + s[5] * b2[at]
            b0[at] = r
            b1[at] = r + s[3] * way
    mass(b1, b2)
    mass(b2, b3)
    mass(b0, b4)
    rr, pm, rm, mm, rmr, mmm, rmm = products(1, [(0, 0), (1, 2), (0, 2), (2, 2), (0, 4), (2, 3), (0, 3)])
    step2 = rr / pm
    norm3 = rr - 2.0 * step2 * rm + step2 * step2 * mm
    share2 = norm3 / rr
    curve = (rmr + step2 * step2 * mmm + share2 * share2 * pm - 2.0 * step2 * rmm + 2.0 * share2 * rm
             - 2.0 * step2 * share2 * mm)
    step3 = norm3 / curve
    for c in range(3):
        s2, s3, h2 = (v[c : c + 1] for v in (step2, step3, share2))
        for q, big_x in every:
            at = (q, big_x, c, slice(None), slice(0, cz))
            p, m = b1[at], b2[at]
            r = b0[at] - s2 * m
            way = r + h2 * p
            ans[q, big_x, c] = ans[q, big_x, c] + s2 * p + s3 * way
            b0[at] = r - s3 * (b4[at] - s2 * b3[at] + h2 * m)

    span = 2 * cy
    for o, source in enumerate((ans, b0)):
        for c in range(3):
            for q, big_x in every:
                for y in range(cy):
                    row = ((o * 3 + c) * nodes_x + big_x) * span + 2 * y + q // 2
                    z = (q % 2) * cz
                    woven[row : row + 1, z : z + cz] = source[q, big_x, c, y : y + 1, :cz]
    lines = lax.broadcasted_iota(jnp.int32, (2 * cz, 2 * cz), 0)
    columns = lax.broadcasted_iota(jnp.int32, (2 * cz, 2 * cz), 1)
    spot = jnp.where(lines < cz, 2 * lines, 2 * (lines - cz) + 1)
    weave = jnp.where(spot == columns, 1.0, 0.0)
    result = jnp.dot(woven[...], weave, precision=lax.Precision.HIGHEST, preferred_element_type=F32)
    for o, target in enumerate((sol_ref, res_ref)):
        for c in range(3):
            for big_x in range(nodes_x):
                row = ((o * 3 + c) * nodes_x + big_x) * span
                target[c, big_x] = result[row : row + span]


def on_device(olds, news, old_field, pair_dest, pair_new, pair_old, pair_block, basis_old, basis_new, volume):
    devices = olds * news
    pairs = pair_dest.shape[0]
    cap = 4 * pairs // devices
    cells = volume.shape
    elements = math.prod(cells)
    smem = pl.BlockSpec(memory_space=pltpu.SMEM)
    vmem = pl.BlockSpec(memory_space=VMEM)
    outgoing = pl.pallas_call(
        functools.partial(pack_kernel, devices, cap),
        out_shape=jax.ShapeDtypeStruct((devices, ROWS, cap), BF16),
        in_specs=[smem] * 4 + [vmem],
        out_specs=vmem,
        scratch_shapes=[
            VMEM((128, old_field.shape[2]), F32),
            VMEM((old_field.shape[2], 128), F32),
            VMEM((devices * cap, 128), F32),
            pltpu.SMEM((devices,), jnp.int32),
        ],
        name="pack",
    )(pair_dest.reshape(-1), pair_new, pair_old, pair_block, old_field)
    kinds = basis_old.shape[0]
    wide = 128 * pl.cdiv(basis_old.shape[2], 128)
    together = 4
    cz = cells[2]
    groups = cz // EDGE
    group = pl.cdiv(row_of(2 * cells[0] + 1, 0, 0, 0) + cells[0], groups)
    pay_rows = groups * group
    payload, edge = pl.pallas_call(
        functools.partial(load_kernel, olds, news, cells, cap, together),
        out_shape=(
            jax.ShapeDtypeStruct((pay_rows,) + cells[1:], F32),
            jax.ShapeDtypeStruct((2, group) + cells[1:], F32),
        ),
        in_specs=[vmem] * 4,
        out_specs=(vmem, vmem),
        scratch_shapes=[
            VMEM((ROWS, devices * cap), BF16),
            VMEM((kinds * ROWS, 3 * wide), F32),
            VMEM((3 * wide, kinds * ROWS), BF16),
            VMEM((kinds * ROWS, 3 * wide), BF16),
            VMEM((2 * ROWS, elements), F32),
            VMEM((ROWS, elements), F32),
            pltpu.SemaphoreType.DMA((devices,)),
            pltpu.SemaphoreType.DMA((devices,)),
        ],
        compiler_params=pltpu.CompilerParams(collective_id=0, has_side_effects=True),
        name="load",
    )(outgoing, jnp.transpose(basis_old, (1, 0, 2)), jnp.transpose(basis_new, (1, 0, 2)), volume)
    nodes_x = 2 * cells[0] + 1
    ny = olds * cells[1]
    grid = (4, nodes_x, 3)
    own = jax.ShapeDtypeStruct((3, nodes_x, 2 * cells[1], 2 * cz), F32)
    return pl.pallas_call(
        functools.partial(solve_kernel, olds, news, cells),
        out_shape=(own, own),
        in_specs=[vmem, vmem],
        out_specs=(vmem, vmem),
        scratch_shapes=[
            VMEM((olds, pay_rows) + cells[1:], F32),
            VMEM((2, olds, group) + cells[1:], F32),
            VMEM((pay_rows, ny, cz), F32),
            VMEM((cells[0], ny, 2 * cz), F32),
        ]
        + [VMEM(grid + (ny, 2 * cz), F32)] * 5
        + [
            VMEM(grid + (ny, cz), F32),
            VMEM((2, 24, cz), F32),
            VMEM((2, news, 24, cz), F32),
            VMEM((2 * 3 * nodes_x * 2 * cells[1], 2 * cz), F32),
            pltpu.SemaphoreType.DMA((olds,)),
            pltpu.SemaphoreType.DMA((olds,)),
            pltpu.SemaphoreType.DMA((2 * olds,)),
            pltpu.SemaphoreType.DMA((2 * olds,)),
            pltpu.SemaphoreType.DMA((2, news)),
            pltpu.SemaphoreType.DMA((2, news)),
        ],
        compiler_params=pltpu.CompilerParams(collective_id=1, has_side_effects=True),
        name="solve",
    )(payload, edge)


def solution(mesh):
    in_specs = (
        P(None, None, ("old", "new")),
        P(("old", "new"), None),
        P(("old", "new")),
        P(("old", "new")),
        P(("old", "new")),
        P(),
        P(),
        P(None, "old", "new"),
    )
    out_specs = (P(None, None, "old", "new"), P(None, None, "old", "new"))
    return jax.shard_map(
        functools.partial(on_device, mesh.shape["old"], mesh.shape["new"]),
        mesh=mesh,
        in_specs=in_specs,
        out_specs=out_specs,
        check_vma=False,
    )
```
